32 devices in a mesh: shot: 4 (over z), rcv: 8 (over y, x, core).
Axes of the slice: x: 2, y: 2, z: 4, core: 2. Of those that a mesh axis runs over, the one named last changes fastest.
Arguments:
- shot_side: bfloat16 [2, 2048, 1024], P(None, 'shot', 'rcv'), may hold values from -6 to 6
- rcv_side: bfloat16 [1024, 12288], P('shot', 'rcv'), may hold values from -0.125 to 0.125
Outputs:
- multiples: bfloat16 [2048, 12288], P('shot', 'rcv')
The draws below stay inside these ranges and needn't reach their ends.
All inputs are finite; a program needn't handle non-finite values.
Results may differ from the reference program's by a relative error of at most 0.001.
Values may be sent and summed in bfloat16 or wider, within the bound.
No kernel may reach another device: no remote copies, remote signals or barrier semaphores. Data moves between devices by JAX's collectives and lax.ppermute only.
A program may use at most 64 MiB of HBM per device.

```python
import jax
import jax.numpy as jnp

SHOT_DEV = 512
RCV_DEV = 768
KB = 256
STEPS = 4
SHOTS = 2048
RCVS = 6144
SURF = 1024


def block_levels(rng, extent, shards, least, top_value):
    level = 1.0
    for axis_at, parts in shards:
        steps = jax.random.uniform(jax.random.fold_in(jax.random.fold_in(rng, 6), axis_at), (parts,), jnp.float32, least / len(shards), top_value / len(shards))
        level = level * jnp.repeat(jnp.exp(steps), extent[axis_at] // parts).reshape((-1,) + (1,) * (len(extent) - 1 - axis_at))
    return level


def bell_draw(own_key, extent, width, bound, pieces=(), dtype=jnp.bfloat16):
    factor_of = block_levels(own_key, extent, pieces, -0.22, 0.18) if pieces else 1.0
    array = jax.random.normal(own_key, extent, jnp.float32) * width * factor_of
    return jnp.minimum(jnp.maximum(array, -bound), bound).astype(dtype)


def setup_inputs(seed: int = 0) -> dict:
    streams_of = jax.random.split(jax.random.key(seed), 3)
    shot_side = bell_draw(streams_of[0], (2, SHOTS, SURF), 1.0, 6.0, ((1, 4), (2, 8)))
    rcv_side = bell_draw(streams_of[1], (SURF, 2 * RCVS), (2 * STEPS * KB) ** -0.5, 0.125, ((0, 4), (1, 8)))
    return dict(shot_side=shot_side, rcv_side=rcv_side)


def reference(shot_side, rcv_side):
    groups = SHOTS // SHOT_DEV
    blocks = SURF // KB
    runs = RCVS // RCV_DEV
    results = []
    for group in range(groups):
        rows = shot_side[:, group * SHOT_DEV:(group + 1) * SHOT_DEV, :]
        total_re = jnp.zeros((SHOT_DEV, RCVS), jnp.float32)
        total_im = jnp.zeros((SHOT_DEV, RCVS), jnp.float32)
        for step in range(STEPS):
            block_id = (group - step) % blocks
            left = rows[:, :, block_id * KB:(block_id + 1) * KB]
            right = rcv_side[block_id * KB:(block_id + 1) * KB, :].reshape(KB, runs, 2, RCV_DEV)
            right_re = right[:, :, 0, :].reshape(KB, RCVS)
            right_im = right[:, :, 1, :].reshape(KB, RCVS)
            real_rr = jnp.dot(left[0], right_re, preferred_element_type=jnp.float32)
            real_ii = jnp.dot(left[1], right_im, preferred_element_type=jnp.float32)
            imag_ri = jnp.dot(left[0], right_im, preferred_element_type=jnp.float32)
            imag_ir = jnp.dot(left[1], right_re, preferred_element_type=jnp.float32)
            total_re = total_re + (real_rr - real_ii)
            total_im = total_im + (imag_ri + imag_ir)
        joined = jnp.stack([total_re.reshape(SHOT_DEV, runs, RCV_DEV), total_im.reshape(SHOT_DEV, runs, RCV_DEV)], axis=2)
        results.append(joined.reshape(SHOT_DEV, 2 * RCVS))
    return jnp.concatenate(results, axis=0).astype(jnp.bfloat16)
```

```python
import jax
import jax.numpy as jnp
from jax import lax
from jax.experimental import pallas as pl
from jax.experimental.pallas import tpu as pltpu
from jax.sharding import PartitionSpec as P

STEPS = 4
VMEM_LIMIT = 16 * 1024 * 1024


def passed_along(value, axis, steps):
    count = lax.axis_size(axis)
    pairs = [(source, (source + steps) % count) for source in range(count)]
    return lax.ppermute(value, axis, pairs)


def from_root(value, axis, root):
    mine = lax.axis_index(axis) == root
    return lax.psum(jnp.where(mine, value, jnp.zeros_like(value)), axis)


def complex_product(left, right):
    half = right.shape[1] // 2
    first = jnp.dot(left[0], right, preferred_element_type=jnp.float32)
    second = jnp.dot(left[1], right, preferred_element_type=jnp.float32)
    real_part = first[:, :half] - second[:, half:]
    imag_part = first[:, half:] + second[:, :half]
    return jnp.concatenate([real_part, imag_part], axis=1)


def ring_on_device(shot_side, rcv_side):
    cycle_size = lax.axis_size("shot")
    pieces = lax.axis_size("rcv") // cycle_size
    shot_index = lax.axis_index("shot")
    total = jnp.zeros((shot_side.shape[1], rcv_side.shape[1]), jnp.float32)
    current = rcv_side
    for step in range(STEPS):
        if step > 0:
            current = passed_along(current, "shot", 1)
        block_id = (shot_index - step) % cycle_size
        gotten = [
            from_root(shot_side, "rcv", block_id * pieces + piece_id)
            for piece_id in range(pieces)
        ]
        total = total + complex_product(jnp.concatenate(gotten, axis=2), current)
    return total.astype(jnp.bfloat16)


SWAP_OUTER = [(0, 1), (1, 0), (2, 3), (3, 2)]
SWAP_INNER = [(1, 2), (2, 1)]
OUTWARD = [(1, 0), (2, 3)]
ACROSS = [(0, 2), (3, 1)]
CHUNKS = 3


def flipped(value, bit):
    return lax.ppermute(value, "rcv", [(i, i ^ bit) for i in range(8)])


def after(value, *others):
    return lax.optimization_barrier((value, *others))[0]


def over_shot(values, pairs):
    return [lax.ppermute(value, "shot", pairs) for value in values]


def kernel_call(kernel, out_shape, flops, count, **options):
    return pl.pallas_call(
        kernel,
        out_shape=out_shape,
        in_specs=[pl.BlockSpec(memory_space=pltpu.VMEM)] * count,
        out_specs=options.pop("out_specs", pl.BlockSpec(memory_space=pltpu.VMEM)),
        compiler_params=pltpu.CompilerParams(vmem_limit_bytes=VMEM_LIMIT),
        cost_estimate=pl.CostEstimate(flops=flops, bytes_accessed=4 << 20, transcendentals=0),
        **options,
    )


def stack_kernel(own, x, y, d, out):
    rcv = lax.axis_index("rcv")
    core0 = rcv % 2 == 0
    here = rcv // 2

    for rel, source in enumerate((own, x, y, d)):
        blk = here ^ rel

        def body(part, carry):
            m, o = source[part], source[2 + part]
            low = jnp.where(core0, m, o)
            high = jnp.where(core0, o, m)
            both = jnp.concatenate([low, high], axis=1)
            out[blk, part, :, 0:256] = both
            out[blk, 1 - part, :, 256:512] = jnp.where(part == 0, both, -both)
            return carry

        lax.fori_loop(0, 2, body, 0)


def tall(right, at, width):
    half = right.shape[1] // 2
    return jnp.concatenate([right[:, at:at + width], right[:, half + at:half + at + width]], axis=0)


def near_kernel(left, own, near, out):
    z = lax.axis_index("shot")
    half = own.shape[1] // 2
    width = half // CHUNKS
    for i in range(CHUNKS):
        right = jnp.concatenate([tall(own, i * width, width), tall(near, i * width, width)], axis=0)

        def body(part, carry):
            rows = jnp.concatenate([left[z, part], left[z ^ 1, part]], axis=1)
            out[CHUNKS * part + i] = jnp.dot(rows, right, preferred_element_type=jnp.float32)
            return carry

        lax.fori_loop(0, 2, body, 0)


def far_block(which, z):
    low = z < 2
    return jnp.where(low, 2, 1) if which == 0 else jnp.where(low, 3, 0)


def add_far(which, z, first, count, left, acc, from_inner, from_outer, out):
    blk = far_block(which, z)
    inner = (z == 1) | (z == 2)
    half = from_inner.shape[1] // 2
    width = half // count
    for i in range(count):
        right = jnp.where(inner, tall(from_inner, i * width, width), tall(from_outer, i * width, width))

        def body(part, carry):
            at = CHUNKS * part + first + i
            total = acc[at] + jnp.dot(left[blk, part], right, preferred_element_type=jnp.float32)
            out[at] = total.astype(out.dtype)
            return carry

        lax.fori_loop(0, 2, body, 0)


def far_kernel(left, acc, from_inner, from_outer, out):
    z = lax.axis_index("shot")
    add_far(0, z, 0, CHUNKS, left, acc, from_inner, from_outer, out)


def copies_out(buf, out, sem, chunks):
    width = buf.shape[2]
    return [
        pltpu.make_async_copy(buf.at[at], out.at[:, pl.ds(at * width, width)], sem.at[at])
        for at in chunks
    ]


def finish(first, left, acc, pairs, out, buf, sem):
    z = lax.axis_index("shot")
    for i, (from_inner, from_outer) in enumerate(pairs):
        add_far(1, z, first + i, 1, left, acc, from_inner, from_outer, buf)
    copies = copies_out(buf, out, sem, [CHUNKS * part + first + i for part in range(2) for i in range(len(pairs))])
    for copy in copies:
        copy.start()
    for copy in copies:
        copy.wait()


def first_kernel(left, acc, inner_a, outer_a, inner_b, outer_b, out, buf, sem):
    finish(0, left, acc, [(inner_a, outer_a), (inner_b, outer_b)], out, buf, sem)


def last_kernel(left, acc, from_inner, from_outer, _, out, buf, sem):
    finish(CHUNKS - 1, left, acc, [(from_inner, from_outer)], out, buf, sem)


def cut(value):
    half = value.shape[1] // 2
    width = half // CHUNKS
    return [
        jnp.concatenate([value[:, at:at + width], value[:, half + at:half + at + width]], axis=1)
        for at in range(0, half, width)
    ]


def line_on_device(shot_side, rcv_side):
    shots, cols = shot_side.shape[1], rcv_side.shape[1]
    width = cols // 2 // CHUNKS
    m1, = over_shot([rcv_side], SWAP_INNER)
    near, = over_shot([rcv_side], SWAP_OUTER)
    m2, = over_shot([rcv_side], ACROSS)
    s2, = over_shot([m1], OUTWARD)
    m2 = cut(m2)
    s3 = over_shot(m2, OUTWARD)

    chip = jnp.concatenate([shot_side, flipped(shot_side, 1)])
    x, y = flipped(chip, 2), flipped(chip, 4)
    x, y, near, m1 = lax.optimization_barrier((x, y, near, m1))
    d = flipped(x, 4)

    left = kernel_call(stack_kernel, jax.ShapeDtypeStruct((4, 2, shots, 512), jnp.bfloat16), 1, 4)(chip, x, y, d)
    block_flops = 8 * shots * 256 * (cols // 2)
    acc_shape = jax.ShapeDtypeStruct((2 * CHUNKS, shots, width), jnp.float32)
    acc = kernel_call(near_kernel, acc_shape, 2 * block_flops, 3)(left, rcv_side, near)
    acc = kernel_call(far_kernel, acc_shape, block_flops, 4)(left, acc, m1, s2)

    out_shape = jax.ShapeDtypeStruct((shots, cols), jnp.bfloat16)
    scratch = [pltpu.VMEM((2 * CHUNKS, shots, width), jnp.bfloat16), pltpu.SemaphoreType.DMA((2 * CHUNKS,))]
    in_place = pl.BlockSpec(memory_space=pl.ANY)
    out = kernel_call(
        first_kernel, out_shape, block_flops * 2 // 3, 6, out_specs=in_place, scratch_shapes=scratch
    )(left, acc, m2[0], s3[0], m2[1], s3[1])
    return pl.pallas_call(
        last_kernel,
        out_shape=out_shape,
        in_specs=[pl.BlockSpec(memory_space=pltpu.VMEM)] * 4 + [in_place],
        out_specs=in_place,
        scratch_shapes=scratch,
        input_output_aliases={4: 0},
        compiler_params=pltpu.CompilerParams(vmem_limit_bytes=VMEM_LIMIT),
        cost_estimate=pl.CostEstimate(flops=block_flops // 3, bytes_accessed=1 << 20, transcendentals=0),
    )(left, acc, m2[2], s3[2], out)


def solution(mesh):
    line = mesh.shape["shot"] == 4 and mesh.shape["rcv"] == 8 and STEPS == 4
    return jax.shard_map(
        line_on_device if line else ring_on_device,
        mesh=mesh,
        in_specs=(P(None, "shot", "rcv"), P("shot", "rcv")),
        out_specs=P("shot", "rcv"),
        check_vma=False,
    )
```

```python
import jax
import jax.numpy as jnp
from jax import lax
from jax.experimental import pallas as pl
from jax.experimental.pallas import tpu as pltpu
from jax.sharding import PartitionSpec as P

STEPS = 4
VMEM_LIMIT = 16 * 1024 * 1024


def passed_along(value, axis, steps):
    count = lax.axis_size(axis)
    pairs = [(source, (source + steps) % count) for source in range(count)]
    return lax.ppermute(value, axis, pairs)


def from_root(value, axis, root):
    mine = lax.axis_index(axis) == root
    return lax.psum(jnp.where(mine, value, jnp.zeros_like(value)), axis)


def complex_product(left, right):
    half = right.shape[1] // 2
    first = jnp.dot(left[0], right, preferred_element_type=jnp.float32)
    second = jnp.dot(left[1], right, preferred_element_type=jnp.float32)
    real_part = first[:, :half] - second[:, half:]
    imag_part = first[:, half:] + second[:, :half]
    return jnp.concatenate([real_part, imag_part], axis=1)


def ring_on_device(shot_side, rcv_side):
    cycle_size = lax.axis_size("shot")
    pieces = lax.axis_size("rcv") // cycle_size
    shot_index = lax.axis_index("shot")
    total = jnp.zeros((shot_side.shape[1], rcv_side.shape[1]), jnp.float32)
    current = rcv_side
    for step in range(STEPS):
        if step > 0:
            current = passed_along(current, "shot", 1)
        block_id = (shot_index - step) % cycle_size
        gotten = [
            from_root(shot_side, "rcv", block_id * pieces + piece_id)
            for piece_id in range(pieces)
        ]
        total = total + complex_product(jnp.concatenate(gotten, axis=2), current)
    return total.astype(jnp.bfloat16)


SWAP_OUTER = [(0, 1), (1, 0), (2, 3), (3, 2)]
SWAP_INNER = [(8 * z + q, 8 * (3 - z) + q if z in (1, 2) else 8 * z + (q ^ 1)) for z in range(4) for q in range(8)]
OUTWARD = [(1, 0), (2, 3)]
ACROSS = [(0, 2), (3, 1)]
CHUNKS = 3


def flipped(value, bit):
    return lax.ppermute(value, "rcv", [(i, i ^ bit) for i in range(8)])


def after(value, *others):
    return lax.optimization_barrier((value, *others))[0]


def over_shot(values, pairs):
    return [lax.ppermute(value, "shot", pairs) for value in values]


def kernel_call(kernel, out_shape, flops, count, **options):
    return pl.pallas_call(
        kernel,
        out_shape=out_shape,
        in_specs=[pl.BlockSpec(memory_space=pltpu.VMEM)] * count,
        out_specs=options.pop("out_specs", pl.BlockSpec(memory_space=pltpu.VMEM)),
        compiler_params=pltpu.CompilerParams(vmem_limit_bytes=VMEM_LIMIT),
        cost_estimate=pl.CostEstimate(flops=flops, bytes_accessed=4 << 20, transcendentals=0),
        **options,
    )


def stack_kernel(own, x, y, d, out):
    rcv = lax.axis_index("rcv")
    core0 = rcv % 2 == 0
    here = rcv // 2

    for rel, source in enumerate((own, x, y, d)):
        blk = here ^ rel

        def body(part, carry):
            m, o = source[part], source[2 + part]
            low = jnp.where(core0, m, o)
            high = jnp.where(core0, o, m)
            both = jnp.concatenate([low, high], axis=1)
            out[blk, part, :, 0:256] = both
            out[blk, 1 - part, :, 256:512] = jnp.where(part == 0, both, -both)
            return carry

        lax.fori_loop(0, 2, body, 0)


def tall(right, at, width):
    half = right.shape[1] // 2
    return jnp.concatenate([right[:, at:at + width], right[:, half + at:half + at + width]], axis=0)


def near_kernel(left, own, near, out):
    z = lax.axis_index("shot")
    half = own.shape[1] // 2
    width = half // CHUNKS
    for i in range(CHUNKS):
        right = jnp.concatenate([tall(own, i * width, width), tall(near, i * width, width)], axis=0)

        def body(part, carry):
            rows = jnp.concatenate([left[z, part], left[z ^ 1, part]], axis=1)
            out[CHUNKS * part + i] = jnp.dot(rows, right, preferred_element_type=jnp.float32)
            return carry

        lax.fori_loop(0, 2, body, 0)


def far_block(which, z):
    low = z < 2
    return jnp.where(low, 2, 1) if which == 0 else jnp.where(low, 3, 0)


def add_far(which, z, first, count, left, acc, from_inner, from_outer, out):
    blk = far_block(which, z)
    inner = (z == 1) | (z == 2)
    half = from_inner.shape[1] // 2
    width = half // count
    for i in range(count):
        right = jnp.where(inner, tall(from_inner, i * width, width), tall(from_outer, i * width, width))

        def body(part, carry):
            at = CHUNKS * part + first + i
            total = acc[at] + jnp.dot(left[blk, part], right, preferred_element_type=jnp.float32)
            out[at] = total.astype(out.dtype)
            return carry

        lax.fori_loop(0, 2, body, 0)


def far_kernel(left, acc, from_inner, from_outer, out):
    z = lax.axis_index("shot")
    add_far(0, z, 0, CHUNKS, left, acc, from_inner, from_outer, out)


def copies_out(buf, out, sem, chunks):
    width = buf.shape[2]
    return [
        pltpu.make_async_copy(buf.at[at], out.at[:, pl.ds(at * width, width)], sem.at[at])
        for at in chunks
    ]


def finish(first, left, acc, pairs, out, buf, sem):
    z = lax.axis_index("shot")
    for i, (from_inner, from_outer) in enumerate(pairs):
        add_far(1, z, first + i, 1, left, acc, from_inner, from_outer, buf)
    copies = copies_out(buf, out, sem, [CHUNKS * part + first + i for part in range(2) for i in range(len(pairs))])
    for copy in copies:
        copy.start()
    for copy in copies:
        copy.wait()


def first_kernel(left, acc, inner_a, outer_a, inner_b, outer_b, out, buf, sem):
    finish(0, left, acc, [(inner_a, outer_a), (inner_b, outer_b)], out, buf, sem)


def last_kernel(left, acc, from_inner, from_outer, _, out, buf, sem):
    finish(CHUNKS - 1, left, acc, [(from_inner, from_outer)], out, buf, sem)


def cut(value):
    half = value.shape[1] // 2
    width = half // CHUNKS
    return [
        jnp.concatenate([value[:, at:at + width], value[:, half + at:half + at + width]], axis=1)
        for at in range(0, half, width)
    ]


def line_on_device(shot_side, rcv_side):
    shots, cols = shot_side.shape[1], rcv_side.shape[1]
    width = cols // 2 // CHUNKS
    m1 = lax.ppermute(rcv_side, ("shot", "rcv"), SWAP_INNER)
    near, = over_shot([rcv_side], SWAP_OUTER)
    m2, = over_shot([rcv_side], ACROSS)
    s2, = over_shot([m1], OUTWARD)
    m2 = cut(m2)
    s3 = over_shot(m2, OUTWARD)

    chip = jnp.concatenate([shot_side, flipped(shot_side, 1)])
    x, y = flipped(chip, 2), flipped(chip, 4)
    x, y, near, m1 = lax.optimization_barrier((x, y, near, m1))
    d = flipped(x, 4)

    left = kernel_call(stack_kernel, jax.ShapeDtypeStruct((4, 2, shots, 512), jnp.bfloat16), 1, 4)(chip, x, y, d)
    block_flops = 8 * shots * 256 * (cols // 2)
    acc_shape = jax.ShapeDtypeStruct((2 * CHUNKS, shots, width), jnp.float32)
    acc = kernel_call(near_kernel, acc_shape, 2 * block_flops, 3)(left, rcv_side, near)
    acc = kernel_call(far_kernel, acc_shape, block_flops, 4)(left, acc, m1, s2)

    out_shape = jax.ShapeDtypeStruct((shots, cols), jnp.bfloat16)
    scratch = [pltpu.VMEM((2 * CHUNKS, shots, width), jnp.bfloat16), pltpu.SemaphoreType.DMA((2 * CHUNKS,))]
    in_place = pl.BlockSpec(memory_space=pl.ANY)
    out = kernel_call(
        first_kernel, out_shape, block_flops * 2 // 3, 6, out_specs=in_place, scratch_shapes=scratch
    )(left, acc, m2[0], s3[0], m2[1], s3[1])
    return pl.pallas_call(
        last_kernel,
        out_shape=out_shape,
        in_specs=[pl.BlockSpec(memory_space=pltpu.VMEM)] * 4 + [in_place],
        out_specs=in_place,
        scratch_shapes=scratch,
        input_output_aliases={4: 0},
        compiler_params=pltpu.CompilerParams(vmem_limit_bytes=VMEM_LIMIT),
        cost_estimate=pl.CostEstimate(flops=block_flops // 3, bytes_accessed=1 << 20, transcendentals=0),
    )(left, acc, m2[2], s3[2], out)


def solution(mesh):
    line = mesh.shape["shot"] == 4 and mesh.shape["rcv"] == 8 and STEPS == 4
    return jax.shard_map(
        line_on_device if line else ring_on_device,
        mesh=mesh,
        in_specs=(P(None, "shot", "rcv"), P("shot", "rcv")),
        out_specs=P("shot", "rcv"),
        check_vma=False,
    )
```

```python
import jax
import jax.numpy as jnp
from jax import lax
from jax.experimental import pallas as pl
from jax.experimental.pallas import tpu as pltpu
from jax.sharding import PartitionSpec as P

STEPS = 4
VMEM_LIMIT = 16 * 1024 * 1024


def passed_along(value, axis, steps):
    count = lax.axis_size(axis)
    pairs = [(source, (source + steps) % count) for source in range(count)]
    return lax.ppermute(value, axis, pairs)


def from_root(value, axis, root):
    mine = lax.axis_index(axis) == root
    return lax.psum(jnp.where(mine, value, jnp.zeros_like(value)), axis)


def complex_product(left, right):
    half = right.shape[1] // 2
    first = jnp.dot(left[0], right, preferred_element_type=jnp.float32)
    second = jnp.dot(left[1], right, preferred_element_type=jnp.float32)
    real_part = first[:, :half] - second[:, half:]
    imag_part = first[:, half:] + second[:, :half]
    return jnp.concatenate([real_part, imag_part], axis=1)


def ring_on_device(shot_side, rcv_side):
    cycle_size = lax.axis_size("shot")
    pieces = lax.axis_size("rcv") // cycle_size
    shot_index = lax.axis_index("shot")
    total = jnp.zeros((shot_side.shape[1], rcv_side.shape[1]), jnp.float32)
    current = rcv_side
    for step in range(STEPS):
        if step > 0:
            current = passed_along(current, "shot", 1)
        block_id = (shot_index - step) % cycle_size
        gotten = [
            from_root(shot_side, "rcv", block_id * pieces + piece_id)
            for piece_id in range(pieces)
        ]
        total = total + complex_product(jnp.concatenate(gotten, axis=2), current)
    return total.astype(jnp.bfloat16)


SWAP_OUTER = [(0, 1), (1, 0), (2, 3), (3, 2)]
SWAP_INNER = [(8 * z + q, 8 * (3 - z) + q if z in (1, 2) else 8 * z + (q ^ 1)) for z in range(4) for q in range(8)]
OUTWARD = [(1, 0), (2, 3)]
ACROSS = [(0, 2), (3, 1)]
CHUNKS = 3


def after(value, *others):
    return lax.optimization_barrier((value, *others))[0]


def flipped(value, bit):
    return lax.ppermute(value, "rcv", [(i, i ^ bit) for i in range(8)])


def over_shot(value, pairs):
    return lax.ppermute(value, "shot", pairs)


def kernel_call(kernel, out_shape, flops, count, **options):
    return pl.pallas_call(
        kernel,
        out_shape=out_shape,
        in_specs=[pl.BlockSpec(memory_space=pltpu.VMEM)] * count,
        out_specs=options.pop("out_specs", pl.BlockSpec(memory_space=pltpu.VMEM)),
        compiler_params=pltpu.CompilerParams(vmem_limit_bytes=VMEM_LIMIT),
        cost_estimate=pl.CostEstimate(flops=flops, bytes_accessed=4 << 20, transcendentals=0),
        **options,
    )


def stack_kernel(own, x, y, d, out):
    rcv = lax.axis_index("rcv")
    core0 = rcv % 2 == 0
    here = rcv // 2

    for rel, source in enumerate((own, x, y, d)):
        blk = here ^ rel

        def body(part, carry):
            m, o = source[part], source[2 + part]
            low = jnp.where(core0, m, o)
            high = jnp.where(core0, o, m)
            both = jnp.concatenate([low, high], axis=1)
            out[blk, part, :, 0:256] = both
            out[blk, 1 - part, :, 256:512] = jnp.where(part == 0, both, -both)
            return carry

        lax.fori_loop(0, 2, body, 0)


def tall(right, at, width):
    half = right.shape[1] // 2
    return jnp.concatenate([right[:, at:at + width], right[:, half + at:half + at + width]], axis=0)


def far_block(which, z):
    low = z < 2
    return jnp.where(low, 2, 1) if which == 0 else jnp.where(low, 3, 0)


def is_inner(z):
    return (z == 1) | (z == 2)


def most_kernel(left, own, near, from_inner, from_outer, out):
    z = lax.axis_index("shot")
    inner = is_inner(z)
    blk = far_block(0, z)
    width = own.shape[1] // 2 // CHUNKS
    for i in range(CHUNKS):
        at = i * width
        far = jnp.where(inner, tall(from_inner, at, width), tall(from_outer, at, width))
        right = jnp.concatenate([tall(own, at, width), tall(near, at, width), far], axis=0)

        def body(part, carry):
            rows = jnp.concatenate([left[z, part], left[z ^ 1, part], left[blk, part]], axis=1)
            out[CHUNKS * part + i] = jnp.dot(rows, right, preferred_element_type=jnp.float32)
            return carry

        lax.fori_loop(0, 2, body, 0)


def finish(first, pairs, left, acc, out, buf, sem):
    z = lax.axis_index("shot")
    inner = is_inner(z)
    blk = far_block(1, z)
    rows, width = acc.shape[1] // 2, acc.shape[2]
    copies = []
    for i, (from_inner, from_outer) in enumerate(pairs):
        right = jnp.where(inner, tall(from_inner, 0, width), tall(from_outer, 0, width))
        for part in range(2):
            slab = CHUNKS * part + first + i
            for r in range(2):
                these = pl.ds(r * rows, rows)
                total = acc[slab, these] + jnp.dot(left[blk, part, these], right, preferred_element_type=jnp.float32)
                buf[slab, these] = total.astype(buf.dtype)
                copy = pltpu.make_async_copy(
                    buf.at[slab, these], out.at[these, pl.ds(slab * width, width)], sem.at[2 * slab + r]
                )
                copy.start()
                copies.append(copy)
    for copy in copies:
        copy.wait()


def first_kernel(left, acc, inner_a, outer_a, inner_b, outer_b, out, buf, sem):
    finish(0, [(inner_a, outer_a), (inner_b, outer_b)], left, acc, out, buf, sem)


def last_kernel(left, acc, from_inner, from_outer, _, out, buf, sem):
    finish(CHUNKS - 1, [(from_inner, from_outer)], left, acc, out, buf, sem)


def cut(value, parts, total=CHUNKS):
    half = value.shape[1] // 2
    width = half // total
    out, at = [], 0
    for count in parts:
        low, high = at * width, (at + count) * width
        out.append(value if count == total else jnp.concatenate([value[:, low:high], value[:, half + low:half + high]], axis=1))
        at += count
    return out


def line_on_device(shot_side, rcv_side):
    shots, cols = shot_side.shape[1], rcv_side.shape[1]
    width = cols // 2 // CHUNKS

    near = over_shot(rcv_side, SWAP_OUTER)
    mid = lax.ppermute(rcv_side, ("shot", "rcv"), SWAP_INNER)

    core = flipped(shot_side, 1)
    chip = jnp.concatenate([shot_side, core])
    x, y = flipped(chip, 2), flipped(chip, 4)
    diag = flipped(after(x, y, near, mid), 4)

    outer_mid = over_shot(mid, OUTWARD)
    across_a, across_b = cut(rcv_side, (2, 1))
    across_a = over_shot(after(across_a, core), ACROSS)
    across_b = over_shot(across_b, ACROSS)
    inner = cut(across_a, (1, 1), 2) + [across_b]
    outer_a = over_shot(inner[0], OUTWARD)
    outer_b = over_shot(after(inner[1], near, diag), OUTWARD)
    outer_c = over_shot(after(inner[2], near, outer_a), OUTWARD)

    left = kernel_call(stack_kernel, jax.ShapeDtypeStruct((4, 2, shots, 512), jnp.bfloat16), 1, 4)(chip, x, y, diag)
    block_flops = 8 * shots * 256 * (cols // 2)
    acc_shape = jax.ShapeDtypeStruct((2 * CHUNKS, shots, width), jnp.float32)
    acc = kernel_call(most_kernel, acc_shape, 3 * block_flops, 5)(left, rcv_side, near, mid, outer_mid)

    out_shape = jax.ShapeDtypeStruct((shots, cols), jnp.bfloat16)
    scratch = [pltpu.VMEM((2 * CHUNKS, shots, width), jnp.bfloat16), pltpu.SemaphoreType.DMA((4 * CHUNKS,))]
    in_place = pl.BlockSpec(memory_space=pl.ANY)
    out = kernel_call(
        first_kernel, out_shape, block_flops * 2 // 3, 6, out_specs=in_place, scratch_shapes=scratch
    )(left, acc, inner[0], outer_a, inner[1], outer_b)
    return pl.pallas_call(
        last_kernel,
        out_shape=out_shape,
        in_specs=[pl.BlockSpec(memory_space=pltpu.VMEM)] * 4 + [in_place],
        out_specs=in_place,
        scratch_shapes=scratch,
        input_output_aliases={4: 0},
        compiler_params=pltpu.CompilerParams(vmem_limit_bytes=VMEM_LIMIT),
        cost_estimate=pl.CostEstimate(flops=block_flops // 3, bytes_accessed=1 << 20, transcendentals=0),
    )(left, acc, inner[2], outer_c, out)


def solution(mesh):
    line = mesh.shape["shot"] == 4 and mesh.shape["rcv"] == 8 and STEPS == 4
    return jax.shard_map(
        line_on_device if line else ring_on_device,
        mesh=mesh,
        in_specs=(P(None, "shot", "rcv"), P("shot", "rcv")),
        out_specs=P("shot", "rcv"),
        check_vma=False,
    )
```

```python
import jax
import jax.numpy as jnp
from jax import lax
from jax.experimental import pallas as pl
from jax.experimental.pallas import tpu as pltpu
from jax.sharding import PartitionSpec as P

STEPS = 4
VMEM_LIMIT = 16 * 1024 * 1024


def passed_along(value, axis, steps):
    count = lax.axis_size(axis)
    pairs = [(source, (source + steps) % count) for source in range(count)]
    return lax.ppermute(value, axis, pairs)


def from_root(value, axis, root):
    mine = lax.axis_index(axis) == root
    return lax.psum(jnp.where(mine, value, jnp.zeros_like(value)), axis)


def complex_product(left, right):
    half = right.shape[1] // 2
    first = jnp.dot(left[0], right, preferred_element_type=jnp.float32)
    second = jnp.dot(left[1], right, preferred_element_type=jnp.float32)
    real_part = first[:, :half] - second[:, half:]
    imag_part = first[:, half:] + second[:, :half]
    return jnp.concatenate([real_part, imag_part], axis=1)


def ring_on_device(shot_side, rcv_side):
    cycle_size = lax.axis_size("shot")
    pieces = lax.axis_size("rcv") // cycle_size
    shot_index = lax.axis_index("shot")
    total = jnp.zeros((shot_side.shape[1], rcv_side.shape[1]), jnp.float32)
    current = rcv_side
    for step in range(STEPS):
        if step > 0:
            current = passed_along(current, "shot", 1)
        block_id = (shot_index - step) % cycle_size
        gotten = [
            from_root(shot_side, "rcv", block_id * pieces + piece_id)
            for piece_id in range(pieces)
        ]
        total = total + complex_product(jnp.concatenate(gotten, axis=2), current)
    return total.astype(jnp.bfloat16)


SWAP_OUTER = [(0, 1), (1, 0), (2, 3), (3, 2)]
SWAP_INNER = [(8 * z + q, 8 * (3 - z) + q if z in (1, 2) else 8 * z + (q ^ 1)) for z in range(4) for q in range(8)]
OUTWARD = [(1, 0), (2, 3)]
ACROSS = [(0, 2), (3, 1)]
CHUNKS = 3


def after(value, *others):
    return lax.optimization_barrier((value, *others))[0]


def flipped(value, bit):
    return lax.ppermute(value, "rcv", [(i, i ^ bit) for i in range(8)])


def over_shot(value, pairs):
    return lax.ppermute(value, "shot", pairs)


def kernel_call(kernel, out_shape, flops, count, **options):
    return pl.pallas_call(
        kernel,
        out_shape=out_shape,
        in_specs=[pl.BlockSpec(memory_space=pltpu.VMEM)] * count,
        out_specs=options.pop("out_specs", pl.BlockSpec(memory_space=pltpu.VMEM)),
        compiler_params=pltpu.CompilerParams(vmem_limit_bytes=VMEM_LIMIT),
        cost_estimate=pl.CostEstimate(flops=flops, bytes_accessed=4 << 20, transcendentals=0),
        **options,
    )


def stack_kernel(own, x, y, d, out):
    rcv = lax.axis_index("rcv")
    core0 = rcv % 2 == 0
    here = rcv // 2

    for rel, source in enumerate((own, x, y, d)):
        blk = here ^ rel

        def body(part, carry):
            m, o = source[part], source[2 + part]
            low = jnp.where(core0, m, o)
            high = jnp.where(core0, o, m)
            both = jnp.concatenate([low, high], axis=1)
            out[blk, part, :, 0:256] = both
            out[blk, 1 - part, :, 256:512] = jnp.where(part == 0, both, -both)
            return carry

        lax.fori_loop(0, 2, body, 0)


def tall(right, at, width):
    half = right.shape[1] // 2
    return jnp.concatenate([right[:, at:at + width], right[:, half + at:half + at + width]], axis=0)


def far_block(which, z):
    low = z < 2
    return jnp.where(low, 2, 1) if which == 0 else jnp.where(low, 3, 0)


def is_inner(z):
    return (z == 1) | (z == 2)


def most_kernel(left, own, near, inner_a, outer_a, inner_b, outer_b, out):
    z = lax.axis_index("shot")
    inner = is_inner(z)
    blk = far_block(0, z)
    width = own.shape[1] // 2 // CHUNKS
    for i in range(CHUNKS):
        at = i * width
        first, second, start = (inner_a, outer_a, at) if i < 2 else (inner_b, outer_b, 0)
        far = jnp.where(inner, tall(first, start, width), tall(second, start, width))
        right = jnp.concatenate([tall(own, at, width), tall(near, at, width), far], axis=0)

        def body(part, carry):
            rows = jnp.concatenate([left[z, part], left[z ^ 1, part], left[blk, part]], axis=1)
            out[CHUNKS * part + i] = jnp.dot(rows, right, preferred_element_type=jnp.float32)
            return carry

        lax.fori_loop(0, 2, body, 0)


def finish(first, pairs, left, acc, out, buf, sem):
    z = lax.axis_index("shot")
    inner = is_inner(z)
    blk = far_block(1, z)
    rows, width = acc.shape[1] // 2, acc.shape[2]
    copies = []
    for i, (from_inner, from_outer) in enumerate(pairs):
        right = jnp.where(inner, tall(from_inner, 0, width), tall(from_outer, 0, width))
        for part in range(2):
            slab = CHUNKS * part + first + i
            for r in range(2):
                these = pl.ds(r * rows, rows)
                total = acc[slab, these] + jnp.dot(left[blk, part, these], right, preferred_element_type=jnp.float32)
                buf[slab, these] = total.astype(buf.dtype)
                copy = pltpu.make_async_copy(
                    buf.at[slab, these], out.at[these, pl.ds(slab * width, width)], sem.at[2 * slab + r]
                )
                copy.start()
                copies.append(copy)
    for copy in copies:
        copy.wait()


def first_kernel(left, acc, inner_a, outer_a, inner_b, outer_b, out, buf, sem):
    finish(0, [(inner_a, outer_a), (inner_b, outer_b)], left, acc, out, buf, sem)


def last_kernel(left, acc, from_inner, from_outer, _, out, buf, sem):
    finish(CHUNKS - 1, [(from_inner, from_outer)], left, acc, out, buf, sem)


def cut(value, parts, total=CHUNKS):
    half = value.shape[1] // 2
    width = half // total
    out, at = [], 0
    for count in parts:
        low, high = at * width, (at + count) * width
        out.append(value if count == total else jnp.concatenate([value[:, low:high], value[:, half + low:half + high]], axis=1))
        at += count
    return out


def line_on_device(shot_side, rcv_side):
    shots, cols = shot_side.shape[1], rcv_side.shape[1]
    width = cols // 2 // CHUNKS

    near = over_shot(rcv_side, SWAP_OUTER)
    mid_a, mid_b = (lax.ppermute(piece, ("shot", "rcv"), SWAP_INNER) for piece in cut(rcv_side, (2, 1)))

    core = flipped(shot_side, 1)
    chip = jnp.concatenate([shot_side, core])
    x, y = flipped(chip, 2), flipped(chip, 4)
    diag = flipped(after(x, mid_a, mid_b), 4)

    outer_mid_a = over_shot(mid_a, OUTWARD)
    outer_mid_b = over_shot(after(mid_b, near, x, y, core), OUTWARD)
    across = cut(rcv_side, (1, 1, 1))
    inner_a = over_shot(after(across[0], near, mid_b, y), ACROSS)
    inner_b = over_shot(after(across[1], mid_b, near, core), ACROSS)
    inner_c = over_shot(after(across[2], near, core), ACROSS)
    outer_a = over_shot(inner_a, OUTWARD)
    outer_b = over_shot(inner_b, OUTWARD)
    outer_c = over_shot(after(inner_c, diag, mid_a, outer_mid_a, outer_mid_b), OUTWARD)

    left = kernel_call(stack_kernel, jax.ShapeDtypeStruct((4, 2, shots, 512), jnp.bfloat16), 1, 4)(chip, x, y, diag)
    block_flops = 8 * shots * 256 * (cols // 2)
    acc_shape = jax.ShapeDtypeStruct((2 * CHUNKS, shots, width), jnp.float32)
    acc = kernel_call(most_kernel, acc_shape, 3 * block_flops, 7)(
        left, rcv_side, near, mid_a, outer_mid_a, mid_b, outer_mid_b
    )

    out_shape = jax.ShapeDtypeStruct((shots, cols), jnp.bfloat16)
    scratch = [pltpu.VMEM((2 * CHUNKS, shots, width), jnp.bfloat16), pltpu.SemaphoreType.DMA((4 * CHUNKS,))]
    in_place = pl.BlockSpec(memory_space=pl.ANY)
    out = kernel_call(
        first_kernel, out_shape, block_flops * 2 // 3, 6, out_specs=in_place, scratch_shapes=scratch
    )(left, acc, inner_a, outer_a, inner_b, outer_b)
    return pl.pallas_call(
        last_kernel,
        out_shape=out_shape,
        in_specs=[pl.BlockSpec(memory_space=pltpu.VMEM)] * 4 + [in_place],
        out_specs=in_place,
        scratch_shapes=scratch,
        input_output_aliases={4: 0},
        compiler_params=pltpu.CompilerParams(vmem_limit_bytes=VMEM_LIMIT),
        cost_estimate=pl.CostEstimate(flops=block_flops // 3, bytes_accessed=1 << 20, transcendentals=0),
    )(left, acc, inner_c, outer_c, out)


def on_device(shot_side, rcv_side):
    line = (
        STEPS == 4
        and lax.axis_size("shot") == 4
        and lax.axis_size("rcv") == 8
        and shot_side.shape[2] == 128
        and rcv_side.shape[0] == 256
        and rcv_side.shape[1] % (2 * CHUNKS * 128) == 0
    )
    return (line_on_device if line else ring_on_device)(shot_side, rcv_side)


def solution(mesh):
    return jax.shard_map(
        on_device,
        mesh=mesh,
        in_specs=(P(None, "shot", "rcv"), P("shot", "rcv")),
        out_specs=P("shot", "rcv"),
        check_vma=False,
    )
```

```python
import jax
import jax.numpy as jnp
from jax import lax
from jax.experimental import pallas as pl
from jax.experimental.pallas import tpu as pltpu
from jax.sharding import PartitionSpec as P

STEPS = 4
VMEM_LIMIT = 16 * 1024 * 1024


def passed_along(value, axis, steps):
    count = lax.axis_size(axis)
    pairs = [(source, (source + steps) % count) for source in range(count)]
    return lax.ppermute(value, axis, pairs)


def from_root(value, axis, root):
    mine = lax.axis_index(axis) == root
    return lax.psum(jnp.where(mine, value, jnp.zeros_like(value)), axis)


def complex_product(left, right):
    half = right.shape[1] // 2
    first = jnp.dot(left[0], right, preferred_element_type=jnp.float32)
    second = jnp.dot(left[1], right, preferred_element_type=jnp.float32)
    real_part = first[:, :half] - second[:, half:]
    imag_part = first[:, half:] + second[:, :half]
    return jnp.concatenate([real_part, imag_part], axis=1)


def ring_on_device(shot_side, rcv_side):
    cycle_size = lax.axis_size("shot")
    pieces = lax.axis_size("rcv") // cycle_size
    shot_index = lax.axis_index("shot")
    total = jnp.zeros((shot_side.shape[1], rcv_side.shape[1]), jnp.float32)
    current = rcv_side
    for step in range(STEPS):
        if step > 0:
            current = passed_along(current, "shot", 1)
        block_id = (shot_index - step) % cycle_size
        gotten = [
            from_root(shot_side, "rcv", block_id * pieces + piece_id)
            for piece_id in range(pieces)
        ]
        total = total + complex_product(jnp.concatenate(gotten, axis=2), current)
    return total.astype(jnp.bfloat16)


SWAP_OUTER = [(0, 1), (1, 0), (2, 3), (3, 2)]
SWAP_INNER = [(8 * z + q, 8 * (3 - z) + q if z in (1, 2) else 8 * z + (q ^ 1)) for z in range(4) for q in range(8)]
OUTWARD = [(1, 0), (2, 3)]
ACROSS = [(0, 2), (3, 1)]
CHUNKS = 3


def after(value, *others):
    return lax.optimization_barrier((value, *others))[0]


def flipped(value, bit):
    return lax.ppermute(value, "rcv", [(i, i ^ bit) for i in range(8)])


def over_shot(value, pairs):
    return lax.ppermute(value, "shot", pairs)


def kernel_call(kernel, out_shape, flops, count, **options):
    return pl.pallas_call(
        kernel,
        out_shape=out_shape,
        in_specs=[pl.BlockSpec(memory_space=pltpu.VMEM)] * count,
        out_specs=options.pop("out_specs", pl.BlockSpec(memory_space=pltpu.VMEM)),
        compiler_params=pltpu.CompilerParams(vmem_limit_bytes=VMEM_LIMIT),
        cost_estimate=pl.CostEstimate(flops=flops, bytes_accessed=4 << 20, transcendentals=0),
        **options,
    )


def stack_kernel(own, x, y, d, out):
    rcv = lax.axis_index("rcv")
    core0 = rcv % 2 == 0
    here = rcv // 2

    for rel, source in enumerate((own, x, y, d)):
        blk = here ^ rel

        def body(part, carry):
            m, o = source[part], source[2 + part]
            low = jnp.where(core0, m, o)
            high = jnp.where(core0, o, m)
            both = jnp.concatenate([low, high], axis=1)
            out[blk, part, :, 0:256] = both
            out[blk, 1 - part, :, 256:512] = jnp.where(part == 0, both, -both)
            return carry

        lax.fori_loop(0, 2, body, 0)


def tall(right, at, width):
    half = right.shape[1] // 2
    return jnp.concatenate([right[:, at:at + width], right[:, half + at:half + at + width]], axis=0)


def far_block(which, z):
    low = z < 2
    return jnp.where(low, 2, 1) if which == 0 else jnp.where(low, 3, 0)


def is_inner(z):
    return (z == 1) | (z == 2)


def most_kernel(left, own, near, from_inner, from_outer, out):
    z = lax.axis_index("shot")
    inner = is_inner(z)
    blk = far_block(0, z)
    width = own.shape[1] // 2 // CHUNKS
    for i in range(CHUNKS):
        at = i * width
        far = jnp.where(inner, tall(from_inner, at, width), tall(from_outer, at, width))
        right = jnp.concatenate([tall(own, at, width), tall(near, at, width), far], axis=0)

        def body(part, carry):
            rows = jnp.concatenate([left[z, part], left[z ^ 1, part], left[blk, part]], axis=1)
            out[CHUNKS * part + i] = jnp.dot(rows, right, preferred_element_type=jnp.float32)
            return carry

        lax.fori_loop(0, 2, body, 0)


def finish(first, pairs, left, acc, out, buf, sem):
    z = lax.axis_index("shot")
    inner = is_inner(z)
    blk = far_block(1, z)
    rows, width = acc.shape[1] // 2, acc.shape[2]
    copies = []
    for i, (from_inner, from_outer) in enumerate(pairs):
        right = jnp.where(inner, tall(from_inner, 0, width), tall(from_outer, 0, width))
        for part in range(2):
            slab = CHUNKS * part + first + i
            for r in range(2):
                these = pl.ds(r * rows, rows)
                total = acc[slab, these] + jnp.dot(left[blk, part, these], right, preferred_element_type=jnp.float32)
                buf[slab, these] = total.astype(buf.dtype)
                copy = pltpu.make_async_copy(
                    buf.at[slab, these], out.at[these, pl.ds(slab * width, width)], sem.at[2 * slab + r]
                )
                copy.start()
                copies.append(copy)
    for copy in copies:
        copy.wait()


def first_kernel(left, acc, inner_a, outer_a, inner_b, outer_b, out, buf, sem):
    finish(0, [(inner_a, outer_a), (inner_b, outer_b)], left, acc, out, buf, sem)


def last_kernel(left, acc, from_inner, from_outer, _, out, buf, sem):
    finish(CHUNKS - 1, [(from_inner, from_outer)], left, acc, out, buf, sem)


def cut(value, parts, total=CHUNKS):
    half = value.shape[1] // 2
    width = half // total
    out, at = [], 0
    for count in parts:
        low, high = at * width, (at + count) * width
        out.append(value if count == total else jnp.concatenate([value[:, low:high], value[:, half + low:half + high]], axis=1))
        at += count
    return out


def line_on_device(shot_side, rcv_side):
    shots, cols = shot_side.shape[1], rcv_side.shape[1]
    width = cols // 2 // CHUNKS

    near = over_shot(rcv_side, SWAP_OUTER)
    mid = lax.ppermute(rcv_side, ("shot", "rcv"), SWAP_INNER)

    core = flipped(shot_side, 1)
    chip = jnp.concatenate([shot_side, core])
    x, y = flipped(after(chip, core), 2), flipped(chip, 4)
    diag = flipped(after(x, y, near, mid), 4)

    outer_mid = over_shot(after(mid, core), OUTWARD)
    across = cut(rcv_side, (1, 1, 1))
    inner_a = over_shot(across[0], ACROSS)
    inner_b = over_shot(across[1], ACROSS)
    inner_c = over_shot(after(across[2], inner_a), ACROSS)
    outer_a = over_shot(after(inner_a, mid), OUTWARD)
    outer_b = over_shot(after(inner_b, near, outer_mid), OUTWARD)
    outer_c = over_shot(inner_c, OUTWARD)

    left = kernel_call(stack_kernel, jax.ShapeDtypeStruct((4, 2, shots, 512), jnp.bfloat16), 1, 4)(chip, x, y, diag)
    block_flops = 8 * shots * 256 * (cols // 2)
    acc_shape = jax.ShapeDtypeStruct((2 * CHUNKS, shots, width), jnp.float32)
    acc = kernel_call(most_kernel, acc_shape, 3 * block_flops, 5)(left, rcv_side, near, mid, outer_mid)

    out_shape = jax.ShapeDtypeStruct((shots, cols), jnp.bfloat16)
    scratch = [pltpu.VMEM((2 * CHUNKS, shots, width), jnp.bfloat16), pltpu.SemaphoreType.DMA((4 * CHUNKS,))]
    in_place = pl.BlockSpec(memory_space=pl.ANY)
    out = kernel_call(
        first_kernel, out_shape, block_flops * 2 // 3, 6, out_specs=in_place, scratch_shapes=scratch
    )(left, acc, inner_a, outer_a, inner_b, outer_b)
    return pl.pallas_call(
        last_kernel,
        out_shape=out_shape,
        in_specs=[pl.BlockSpec(memory_space=pltpu.VMEM)] * 4 + [in_place],
        out_specs=in_place,
        scratch_shapes=scratch,
        input_output_aliases={4: 0},
        compiler_params=pltpu.CompilerParams(vmem_limit_bytes=VMEM_LIMIT),
        cost_estimate=pl.CostEstimate(flops=block_flops // 3, bytes_accessed=1 << 20, transcendentals=0),
    )(left, acc, inner_c, outer_c, out)


def on_device(shot_side, rcv_side):
    line = (
        STEPS == 4
        and lax.axis_size("shot") == 4
        and lax.axis_size("rcv") == 8
        and shot_side.shape[2] == 128
        and rcv_side.shape[0] == 256
        and rcv_side.shape[1] % (2 * CHUNKS * 128) == 0
    )
    return (line_on_device if line else ring_on_device)(shot_side, rcv_side)


def solution(mesh):
    return jax.shard_map(
        on_device,
        mesh=mesh,
        in_specs=(P(None, "shot", "rcv"), P("shot", "rcv")),
        out_specs=P("shot", "rcv"),
        check_vma=False,
    )
```

```python
import jax
import jax.numpy as jnp
from jax import lax
from jax.experimental import pallas as pl
from jax.experimental.pallas import tpu as pltpu
from jax.sharding import PartitionSpec as P

STEPS = 4
VMEM_LIMIT = 16 * 1024 * 1024


def passed_along(value, axis, steps):
    count = lax.axis_size(axis)
    pairs = [(source, (source + steps) % count) for source in range(count)]
    return lax.ppermute(value, axis, pairs)


def from_root(value, axis, root):
    mine = lax.axis_index(axis) == root
    return lax.psum(jnp.where(mine, value, jnp.zeros_like(value)), axis)


def complex_product(left, right):
    half = right.shape[1] // 2
    first = jnp.dot(left[0], right, preferred_element_type=jnp.float32)
    second = jnp.dot(left[1], right, preferred_element_type=jnp.float32)
    real_part = first[:, :half] - second[:, half:]
    imag_part = first[:, half:] + second[:, :half]
    return jnp.concatenate([real_part, imag_part], axis=1)


def ring_on_device(shot_side, rcv_side):
    cycle_size = lax.axis_size("shot")
    pieces = lax.axis_size("rcv") // cycle_size
    shot_index = lax.axis_index("shot")
    total = jnp.zeros((shot_side.shape[1], rcv_side.shape[1]), jnp.float32)
    current = rcv_side
    for step in range(STEPS):
        if step > 0:
            current = passed_along(current, "shot", 1)
        block_id = (shot_index - step) % cycle_size
        gotten = [
            from_root(shot_side, "rcv", block_id * pieces + piece_id)
            for piece_id in range(pieces)
        ]
        total = total + complex_product(jnp.concatenate(gotten, axis=2), current)
    return total.astype(jnp.bfloat16)


SWAP_OUTER = [(0, 1), (1, 0), (2, 3), (3, 2)]
SWAP_INNER = [(8 * z + q, 8 * (3 - z) + q if z in (1, 2) else 8 * z + (q ^ 1)) for z in range(4) for q in range(8)]
OUTWARD = [(1, 0), (2, 3)]
ACROSS = [(0, 2), (3, 1)]
CHUNKS = 3


def after(value, *others):
    return lax.optimization_barrier((value, *others))[0]


def flipped(value, bit):
    return lax.ppermute(value, "rcv", [(i, i ^ bit) for i in range(8)])


def over_shot(value, pairs):
    return lax.ppermute(value, "shot", pairs)


def kernel_call(kernel, out_shape, flops, count, **options):
    return pl.pallas_call(
        kernel,
        out_shape=out_shape,
        in_specs=[pl.BlockSpec(memory_space=pltpu.VMEM)] * count,
        out_specs=options.pop("out_specs", pl.BlockSpec(memory_space=pltpu.VMEM)),
        compiler_params=pltpu.CompilerParams(vmem_limit_bytes=VMEM_LIMIT),
        cost_estimate=pl.CostEstimate(flops=flops, bytes_accessed=4 << 20, transcendentals=0),
        **options,
    )


def stack_kernel(own, x, y, d, out):
    rcv = lax.axis_index("rcv")
    core0 = rcv % 2 == 0
    here = rcv // 2

    for rel, source in enumerate((own, x, y, d)):
        blk = here ^ rel

        def body(part, carry):
            m, o = source[part], source[2 + part]
            low = jnp.where(core0, m, o)
            high = jnp.where(core0, o, m)
            both = jnp.concatenate([low, high], axis=1)
            out[blk, part, :, 0:256] = both
            out[blk, 1 - part, :, 256:512] = jnp.where(part == 0, both, -both)
            return carry

        lax.fori_loop(0, 2, body, 0)


def tall(right, at, width):
    half = right.shape[1] // 2
    return jnp.concatenate([right[:, at:at + width], right[:, half + at:half + at + width]], axis=0)


def far_block(which, z):
    low = z < 2
    return jnp.where(low, 2, 1) if which == 0 else jnp.where(low, 3, 0)


def is_inner(z):
    return (z == 1) | (z == 2)


def most_kernel(left, own, near, inner_a, outer_a, inner_b, outer_b, out):
    z = lax.axis_index("shot")
    inner = is_inner(z)
    blk = far_block(0, z)
    width = own.shape[1] // 2 // CHUNKS
    for i in range(CHUNKS):
        at = i * width
        first, second, start = (inner_a, outer_a, at) if i < 2 else (inner_b, outer_b, 0)
        far = jnp.where(inner, tall(first, start, width), tall(second, start, width))
        right = jnp.concatenate([tall(own, at, width), tall(near, at, width), far], axis=0)

        def body(part, carry):
            rows = jnp.concatenate([left[z, part], left[z ^ 1, part], left[blk, part]], axis=1)
            out[CHUNKS * part + i] = jnp.dot(rows, right, preferred_element_type=jnp.float32)
            return carry

        lax.fori_loop(0, 2, body, 0)


def finish(first, pairs, left, acc, out, buf, sem):
    z = lax.axis_index("shot")
    inner = is_inner(z)
    blk = far_block(1, z)
    rows, width = acc.shape[1] // 2, acc.shape[2]
    copies = []
    for i, (from_inner, from_outer) in enumerate(pairs):
        right = jnp.where(inner, tall(from_inner, 0, width), tall(from_outer, 0, width))
        for part in range(2):
            slab = CHUNKS * part + first + i
            for r in range(2):
                these = pl.ds(r * rows, rows)
                total = acc[slab, these] + jnp.dot(left[blk, part, these], right, preferred_element_type=jnp.float32)
                buf[slab, these] = total.astype(buf.dtype)
                copy = pltpu.make_async_copy(
                    buf.at[slab, these], out.at[these, pl.ds(slab * width, width)], sem.at[2 * slab + r]
                )
                copy.start()
                copies.append(copy)
    for copy in copies:
        copy.wait()


def first_kernel(left, acc, inner_a, outer_a, inner_b, outer_b, out, buf, sem):
    finish(0, [(inner_a, outer_a), (inner_b, outer_b)], left, acc, out, buf, sem)


def last_kernel(left, acc, from_inner, from_outer, _, out, buf, sem):
    finish(CHUNKS - 1, [(from_inner, from_outer)], left, acc, out, buf, sem)


def cut(value, parts, total=CHUNKS):
    half = value.shape[1] // 2
    width = half // total
    out, at = [], 0
    for count in parts:
        low, high = at * width, (at + count) * width
        out.append(value if count == total else jnp.concatenate([value[:, low:high], value[:, half + low:half + high]], axis=1))
        at += count
    return out


def line_on_device(shot_side, rcv_side):
    shots, cols = shot_side.shape[1], rcv_side.shape[1]
    width = cols // 2 // CHUNKS

    near = over_shot(rcv_side, SWAP_OUTER)
    mid_a, mid_b = (lax.ppermute(piece, ("shot", "rcv"), SWAP_INNER) for piece in cut(rcv_side, (2, 1)))

    core = flipped(shot_side, 1)
    chip = jnp.concatenate([shot_side, core])
    x, y = flipped(chip, 2), flipped(chip, 4)
    diag = flipped(after(x, mid_a, mid_b), 4)

    outer_mid_a = over_shot(mid_a, OUTWARD)
    outer_mid_b = over_shot(after(mid_b, near), OUTWARD)
    across = cut(rcv_side, (1, 1, 1))
    inner_a = over_shot(after(across[0], near, mid_b, y), ACROSS)
    inner_b = over_shot(after(across[1], mid_b, near, y), ACROSS)
    inner_c = over_shot(after(across[2], mid_b, near, y), ACROSS)
    outer_a = over_shot(inner_a, OUTWARD)
    outer_b = over_shot(inner_b, OUTWARD)
    outer_c = over_shot(after(inner_c, diag, mid_a, outer_mid_a, outer_mid_b), OUTWARD)

    left = kernel_call(stack_kernel, jax.ShapeDtypeStruct((4, 2, shots, 512), jnp.bfloat16), 1, 4)(chip, x, y, diag)
    block_flops = 8 * shots * 256 * (cols // 2)
    acc_shape = jax.ShapeDtypeStruct((2 * CHUNKS, shots, width), jnp.float32)
    acc = kernel_call(most_kernel, acc_shape, 3 * block_flops, 7)(
        left, rcv_side, near, mid_a, outer_mid_a, mid_b, outer_mid_b
    )

    out_shape = jax.ShapeDtypeStruct((shots, cols), jnp.bfloat16)
    scratch = [pltpu.VMEM((2 * CHUNKS, shots, width), jnp.bfloat16), pltpu.SemaphoreType.DMA((4 * CHUNKS,))]
    in_place = pl.BlockSpec(memory_space=pl.ANY)
    out = kernel_call(
        first_kernel, out_shape, block_flops * 2 // 3, 6, out_specs=in_place, scratch_shapes=scratch
    )(left, acc, inner_a, outer_a, inner_b, outer_b)
    return pl.pallas_call(
        last_kernel,
        out_shape=out_shape,
        in_specs=[pl.BlockSpec(memory_space=pltpu.VMEM)] * 4 + [in_place],
        out_specs=in_place,
        scratch_shapes=scratch,
        input_output_aliases={4: 0},
        compiler_params=pltpu.CompilerParams(vmem_limit_bytes=VMEM_LIMIT),
        cost_estimate=pl.CostEstimate(flops=block_flops // 3, bytes_accessed=1 << 20, transcendentals=0),
    )(left, acc, inner_c, outer_c, out)


def on_device(shot_side, rcv_side):
    line = (
        STEPS == 4
        and lax.axis_size("shot") == 4
        and lax.axis_size("rcv") == 8
        and shot_side.shape[2] == 128
        and rcv_side.shape[0] == 256
        and rcv_side.shape[1] % (2 * CHUNKS * 128) == 0
    )
    return (line_on_device if line else ring_on_device)(shot_side, rcv_side)


def solution(mesh):
    return jax.shard_map(
        on_device,
        mesh=mesh,
        in_specs=(P(None, "shot", "rcv"), P("shot", "rcv")),
        out_specs=P("shot", "rcv"),
        check_vma=False,
    )
```

```python
import jax
import jax.numpy as jnp
from jax import lax
from jax.experimental import pallas as pl
from jax.experimental.pallas import tpu as pltpu
from jax.sharding import PartitionSpec as P

STEPS = 4
VMEM_LIMIT = 16 * 1024 * 1024


def passed_along(value, axis, steps):
    count = lax.axis_size(axis)
    pairs = [(source, (source + steps) % count) for source in range(count)]
    return lax.ppermute(value, axis, pairs)


def from_root(value, axis, root):
    mine = lax.axis_index(axis) == root
    return lax.psum(jnp.where(mine, value, jnp.zeros_like(value)), axis)


def complex_product(left, right):
    half = right.shape[1] // 2
    first = jnp.dot(left[0], right, preferred_element_type=jnp.float32)
    second = jnp.dot(left[1], right, preferred_element_type=jnp.float32)
    real_part = first[:, :half] - second[:, half:]
    imag_part = first[:, half:] + second[:, :half]
    return jnp.concatenate([real_part, imag_part], axis=1)


def ring_on_device(shot_side, rcv_side):
    cycle_size = lax.axis_size("shot")
    pieces = lax.axis_size("rcv") // cycle_size
    shot_index = lax.axis_index("shot")
    total = jnp.zeros((shot_side.shape[1], rcv_side.shape[1]), jnp.float32)
    current = rcv_side
    for step in range(STEPS):
        if step > 0:
            current = passed_along(current, "shot", 1)
        block_id = (shot_index - step) % cycle_size
        gotten = [
            from_root(shot_side, "rcv", block_id * pieces + piece_id)
            for piece_id in range(pieces)
        ]
        total = total + complex_product(jnp.concatenate(gotten, axis=2), current)
    return total.astype(jnp.bfloat16)


SWAP_OUTER = [(0, 1), (1, 0), (2, 3), (3, 2)]
SWAP_INNER = [(8 * z + q, 8 * (3 - z) + q if z in (1, 2) else 8 * z + (q ^ 1)) for z in range(4) for q in range(8)]
OUTWARD = [(1, 0), (2, 3)]
ACROSS = [(0, 2), (3, 1)]
CHUNKS = 3


def after(value, *others):
    return lax.optimization_barrier((value, *others))[0]


def flipped(value, bit):
    return lax.ppermute(value, "rcv", [(i, i ^ bit) for i in range(8)])


def over_shot(value, pairs):
    return lax.ppermute(value, "shot", pairs)


def kernel_call(kernel, out_shape, flops, count, **options):
    return pl.pallas_call(
        kernel,
        out_shape=out_shape,
        in_specs=[pl.BlockSpec(memory_space=pltpu.VMEM)] * count,
        out_specs=options.pop("out_specs", pl.BlockSpec(memory_space=pltpu.VMEM)),
        compiler_params=pltpu.CompilerParams(vmem_limit_bytes=VMEM_LIMIT),
        cost_estimate=pl.CostEstimate(flops=flops, bytes_accessed=4 << 20, transcendentals=0),
        **options,
    )


def stack_kernel(own, x, y, d, out):
    rcv = lax.axis_index("rcv")
    core0 = rcv % 2 == 0
    here = rcv // 2

    for rel, source in enumerate((own, x, y, d)):
        blk = here ^ rel

        def body(part, carry):
            m, o = source[part], source[2 + part]
            low = jnp.where(core0, m, o)
            high = jnp.where(core0, o, m)
            both = jnp.concatenate([low, high], axis=1)
            out[blk, part, :, 0:256] = both
            out[blk, 1 - part, :, 256:512] = jnp.where(part == 0, both, -both)
            return carry

        lax.fori_loop(0, 2, body, 0)


def tall(right, at, width):
    half = right.shape[1] // 2
    return jnp.concatenate([right[:, at:at + width], right[:, half + at:half + at + width]], axis=0)


def far_block(which, z):
    low = z < 2
    return jnp.where(low, 2, 1) if which == 0 else jnp.where(low, 3, 0)


def is_inner(z):
    return (z == 1) | (z == 2)


def most_kernel(left, own, near, inner_a, outer_a, inner_b, outer_b, out):
    z = lax.axis_index("shot")
    inner = is_inner(z)
    blk = far_block(0, z)
    width = own.shape[1] // 2 // CHUNKS
    for i in range(CHUNKS):
        at = i * width
        first, second, start = (inner_a, outer_a, at) if i < 2 else (inner_b, outer_b, 0)
        far = jnp.where(inner, tall(first, start, width), tall(second, start, width))
        right = jnp.concatenate([tall(own, at, width), tall(near, at, width), far], axis=0)

        def body(part, carry):
            rows = jnp.concatenate([left[z, part], left[z ^ 1, part], left[blk, part]], axis=1)
            out[CHUNKS * part + i] = jnp.dot(rows, right, preferred_element_type=jnp.float32)
            return carry

        lax.fori_loop(0, 2, body, 0)


def finish(first, pairs, left, acc, out, buf, sem):
    z = lax.axis_index("shot")
    inner = is_inner(z)
    blk = far_block(1, z)
    rows, width = acc.shape[1] // 2, acc.shape[2]
    copies = []
    for i, (from_inner, from_outer) in enumerate(pairs):
        right = jnp.where(inner, tall(from_inner, 0, width), tall(from_outer, 0, width))
        for part in range(2):
            slab = CHUNKS * part + first + i
            for r in range(2):
                these = pl.ds(r * rows, rows)
                total = acc[slab, these] + jnp.dot(left[blk, part, these], right, preferred_element_type=jnp.float32)
                buf[slab, these] = total.astype(buf.dtype)
                copy = pltpu.make_async_copy(
                    buf.at[slab, these], out.at[these, pl.ds(slab * width, width)], sem.at[2 * slab + r]
                )
                copy.start()
                copies.append(copy)
    for copy in copies:
        copy.wait()


def first_kernel(left, acc, inner_a, outer_a, inner_b, outer_b, out, buf, sem):
    finish(0, [(inner_a, outer_a), (inner_b, outer_b)], left, acc, out, buf, sem)


def last_kernel(left, acc, from_inner, from_outer, _, out, buf, sem):
    finish(CHUNKS - 1, [(from_inner, from_outer)], left, acc, out, buf, sem)


def cut(value, parts, total=CHUNKS):
    half = value.shape[1] // 2
    width = half // total
    out, at = [], 0
    for count in parts:
        low, high = at * width, (at + count) * width
        out.append(value if count == total else jnp.concatenate([value[:, low:high], value[:, half + low:half + high]], axis=1))
        at += count
    return out


def line_on_device(shot_side, rcv_side):
    shots, cols = shot_side.shape[1], rcv_side.shape[1]
    width = cols // 2 // CHUNKS

    near = over_shot(rcv_side, SWAP_OUTER)
    mid_a, mid_b = (lax.ppermute(piece, ("shot", "rcv"), SWAP_INNER) for piece in cut(rcv_side, (2, 1)))

    core = flipped(shot_side, 1)
    chip = jnp.concatenate([shot_side, core])
    x, y = flipped(chip, 2), flipped(chip, 4)
    diag = flipped(after(x, mid_a, mid_b), 4)

    outer_mid_a = over_shot(mid_a, OUTWARD)
    outer_mid_b = over_shot(after(mid_b, near), OUTWARD)
    across = cut(rcv_side, (1, 1, 1))
    inner_a = over_shot(after(across[0], near, mid_b, y), ACROSS)
    inner_b = over_shot(after(across[1], mid_b, near, y), ACROSS)
    inner_c = over_shot(after(across[2], mid_b, near, y), ACROSS)
    outer_a = over_shot(inner_a, OUTWARD)
    outer_b = over_shot(inner_b, OUTWARD)
    outer_c = over_shot(after(inner_c, outer_mid_a, outer_mid_b), OUTWARD)

    left = kernel_call(stack_kernel, jax.ShapeDtypeStruct((4, 2, shots, 512), jnp.bfloat16), 1, 4)(chip, x, y, diag)
    block_flops = 8 * shots * 256 * (cols // 2)
    acc_shape = jax.ShapeDtypeStruct((2 * CHUNKS, shots, width), jnp.float32)
    acc = kernel_call(most_kernel, acc_shape, 3 * block_flops, 7)(
        left, rcv_side, near, mid_a, outer_mid_a, mid_b, outer_mid_b
    )

    out_shape = jax.ShapeDtypeStruct((shots, cols), jnp.bfloat16)
    scratch = [pltpu.VMEM((2 * CHUNKS, shots, width), jnp.bfloat16), pltpu.SemaphoreType.DMA((4 * CHUNKS,))]
    in_place = pl.BlockSpec(memory_space=pl.ANY)
    out = kernel_call(
        first_kernel, out_shape, block_flops * 2 // 3, 6, out_specs=in_place, scratch_shapes=scratch
    )(left, acc, inner_a, outer_a, inner_b, outer_b)
    return pl.pallas_call(
        last_kernel,
        out_shape=out_shape,
        in_specs=[pl.BlockSpec(memory_space=pltpu.VMEM)] * 4 + [in_place],
        out_specs=in_place,
        scratch_shapes=scratch,
        input_output_aliases={4: 0},
        compiler_params=pltpu.CompilerParams(vmem_limit_bytes=VMEM_LIMIT),
        cost_estimate=pl.CostEstimate(flops=block_flops // 3, bytes_accessed=1 << 20, transcendentals=0),
    )(left, acc, inner_c, outer_c, out)


def on_device(shot_side, rcv_side):
    line = (
        STEPS == 4
        and lax.axis_size("shot") == 4
        and lax.axis_size("rcv") == 8
        and shot_side.shape[2] == 128
        and rcv_side.shape[0] == 256
        and rcv_side.shape[1] % (2 * CHUNKS * 128) == 0
    )
    return (line_on_device if line else ring_on_device)(shot_side, rcv_side)


def solution(mesh):
    return jax.shard_map(
        on_device,
        mesh=mesh,
        in_specs=(P(None, "shot", "rcv"), P("shot", "rcv")),
        out_specs=P("shot", "rcv"),
        check_vma=False,
    )
```
